128 devices in a mesh: row: 16 (over x_hi, z, core), col: 8 (over x_lo, y).
Axes of the slice: x: 4 (x_hi: 2, x_lo: 2; x = x_hi * 2 + x_lo), y: 4, z: 4, core: 2. Of those that a mesh axis runs over, the one named last changes fastest.
Arguments:
- approximant: bfloat16 [7168, 7168], P('row', 'col'), may hold values from -2 to 2
Outputs:
- squared: bfloat16 [7168, 7168], P('row', 'col')
- fourth_power: bfloat16 [7168, 7168], P('row', 'col')
The draws below stay inside these ranges and needn't reach their ends.
All inputs are finite; a program needn't handle non-finite values.
Results may differ from the reference program's by a relative error of at most 0.006.
Values may be sent and summed in bfloat16 or wider, within the bound.
No kernel may reach another device: no remote copies, remote signals or barrier semaphores. Data moves between devices by JAX's collectives and lax.ppermute only.
A program may use at most 64 MiB of HBM per device.

```python
import jax
import jax.numpy as jnp
from jax import lax

N = 7168


def draw_approximant(key, part):
    first = jax.random.fold_in(key, 11)
    second = jax.random.fold_in(key, 23)
    spread = 0.5 / N ** 0.5
    offdiag = jnp.clip(jax.random.normal(first, (N, N), jnp.float32), -6.0, 6.0) * spread
    diagonal = jax.random.uniform(second, (N,), jnp.float32, 0.5, 1.5)
    rows = lax.broadcasted_iota(jnp.int32, (N, N), 0)
    columns = lax.broadcasted_iota(jnp.int32, (N, N), 1)
    matrix = jnp.where(rows == columns, diagonal[:, None], offdiag)
    return matrix.astype(jnp.bfloat16)


def setup_inputs(seed: int = 0) -> dict:
    keys = jax.random.split(jax.random.key(seed), 2)
    return {
        "approximant": draw_approximant(jax.random.fold_in(keys[1], 71), 0),
    }


def reference(approximant):
    squared = jnp.dot(approximant, approximant, preferred_element_type=jnp.float32).astype(jnp.bfloat16)
    fourth_power = jnp.dot(squared, squared, preferred_element_type=jnp.float32).astype(jnp.bfloat16)
    return (squared, fourth_power)
```

```python
import jax
import jax.numpy as jnp
from jax import lax
from jax.experimental import pallas as pl
from jax.experimental.pallas import tpu as pltpu
from jax.sharding import PartitionSpec as P


AXES = ("row", "col")
B = 448
W = 896
H = B // 2


def pairs(move):
    out = []
    for xh in range(2):
        for z in range(4):
            for core in range(2):
                for xl in range(2):
                    for y in range(4):
                        a, b, c, d, e = move(xh, z, core, xl, y)
                        source = ((xh * 4 + z) * 2 + core) * 8 + xl * 4 + y
                        target = (((a % 2) * 4 + b % 4) * 2 + c % 2) * 8 + (d % 2) * 4 + e % 4
                        out.append((source, target))
    return out


Y_UP = pairs(lambda xh, z, core, xl, y: (xh, z, core, xl, y + 1))
Y_DOWN = pairs(lambda xh, z, core, xl, y: (xh, z, core, xl, y + 3))
Z_UP = pairs(lambda xh, z, core, xl, y: (xh, z + 1, core, xl, y))
Z_DOWN = pairs(lambda xh, z, core, xl, y: (xh, z + 3, core, xl, y))
X_LO = pairs(lambda xh, z, core, xl, y: (xh, z, core, xl + 1, y))
X_HI = pairs(lambda xh, z, core, xl, y: (xh + 1, z, core, xl, y))
CORE = pairs(lambda xh, z, core, xl, y: (xh, z, core + 1, xl, y))


def send(value, where):
    return lax.ppermute(value, AXES, where)


def ring(own, partner, up, down):
    below = send(own, up)
    above = send(own, down)
    partner_below = send(partner, up)
    partner_above = send(partner, down)
    far_top = send(jnp.concatenate([below[:H], partner_below[:H]], axis=0), up)
    far_bottom = send(jnp.concatenate([above[H:], partner_above[H:]], axis=0), down)
    return [own, above, below, partner, partner_above, partner_below, far_top, far_bottom]


def copies(refs, which, target, at, column, sem):
    own, above, below, partner, partner_above, partner_below, far_top, far_bottom = refs
    whole = {0: own, 1: above, 3: below, 4: partner, 5: partner_above, 7: partner_below}
    cols = pl.ds(column, W)
    for index, ref in whole.items():

        @pl.when(which == index)
        def _(ref=ref):
            pltpu.make_async_copy(ref, target.at[pl.ds(at, B), cols], sem).start()

    for index, off in ((2, 0), (6, H)):

        @pl.when(which == index)
        def _(off=off):
            pltpu.make_async_copy(far_top.at[pl.ds(off, H)], target.at[pl.ds(at, H), cols], sem).start()
            pltpu.make_async_copy(far_bottom.at[pl.ds(off, H)], target.at[pl.ds(at + H, H), cols], sem).start()


def mm_kernel(steps, index_ref, *refs):
    lhs, mine, other = refs[0:8], refs[8:16], refs[16:24]
    out, a, b, acc, sem_a, sem_b = refs[24:]
    core = index_ref[2 * steps]
    at_mine = pl.multiple_of(core * B, B)
    at_other = pl.multiple_of((1 - core) * B, B)
    for t in range(steps):
        copies(lhs, index_ref[t], a, 0, t * W, sem_a.at[t])
        copies(mine, index_ref[steps + t], b, t * W + at_mine, 0, sem_b.at[t])
        copies(other, index_ref[steps + t], b, t * W + at_other, 0, sem_b.at[t])
    for t in range(0, steps, 2):
        for u in (t, t + 1):
            pltpu.make_async_copy(lhs[0], a.at[:, pl.ds(u * W, W)], sem_a.at[u]).wait()
            pltpu.make_async_copy(b.at[pl.ds(u * W, W)], b.at[pl.ds(u * W, W)], sem_b.at[u]).wait()
        part = jnp.dot(a[:, t * W:(t + 2) * W], b[t * W:(t + 2) * W, :], preferred_element_type=jnp.float32)
        if t == 0:
            acc[...] = part
        elif t < steps - 2:
            acc[...] += part
        else:
            out[...] = (acc[...] + part).astype(out.dtype)


def multiply(lhs, mine, other, index):
    steps = 8
    return pl.pallas_call(
        lambda *refs: mm_kernel(steps, *refs),
        out_shape=jax.ShapeDtypeStruct((B, W), jnp.bfloat16),
        in_specs=[pl.BlockSpec(memory_space=pltpu.SMEM)] + [pl.BlockSpec(memory_space=pl.ANY)] * 24,
        out_specs=pl.BlockSpec(memory_space=pltpu.VMEM),
        scratch_shapes=[
            pltpu.VMEM((B, steps * W), jnp.bfloat16),
            pltpu.VMEM((steps * W, W), jnp.bfloat16),
            pltpu.VMEM((B, W), jnp.float32),
            pltpu.SemaphoreType.DMA((steps,)),
            pltpu.SemaphoreType.DMA((steps,)),
        ],
        compiler_params=pltpu.CompilerParams(vmem_limit_bytes=40 << 20),
        cost_estimate=pl.CostEstimate(flops=2 * B * W * W * steps, bytes_accessed=3 * B * W * 2 * steps, transcendentals=0),
    )(index, *lhs, *mine, *other)


def square(block):
    r = lax.axis_index("row")
    c = lax.axis_index("col")
    core = r % 2
    z, xh = (r // 2) % 4, r // 8
    y, xl = c % 4, c // 4
    lhs = ring(block, send(block, X_LO), Y_UP, Y_DOWN)
    mine = ring(block, send(block, X_HI), Z_UP, Z_DOWN)
    other = [send(v, CORE) for v in mine]
    rows, columns = [], []
    for k in range(8):
        hi, lo = k // 4, k % 4
        rows.append((hi ^ xl) * 4 + (lo - y) % 4)
        columns.append((hi ^ xh) * 4 + (lo - z) % 4)
    index = jnp.stack(rows + columns + [core]).astype(jnp.int32)
    return multiply(lhs, mine, other, index)


def body(approximant):
    squared = square(approximant)
    fourth_power = square(squared)
    return (squared, fourth_power)


def solution(mesh):
    return jax.shard_map(
        body,
        mesh=mesh,
        in_specs=(P("row", "col"),),
        out_specs=(P("row", "col"), P("row", "col")),
        check_vma=False,
    )
```

```python
import functools

import jax
import jax.numpy as jnp
import numpy as np
from jax import lax
from jax.experimental import pallas as pl
from jax.experimental.pallas import tpu as pltpu
from jax.sharding import PartitionSpec as P


AXES = ("row", "col")
B = 448
W = 896
GROUPS = ((1, 2), (1,), (1, 2), (1,))


def devices():
    for xh in range(2):
        for z in range(4):
            for core in range(2):
                for xl in range(2):
                    for y in range(4):
                        yield xh, z, core, xl, y


def pairs(move):
    out = []
    for source, place in enumerate(devices()):
        xh, z, core, xl, y = move(*place)
        out.append((source, (((xh % 2) * 4 + z % 4) * 2 + core % 2) * 8 + (xl % 2) * 4 + y % 4))
    return out


Y_UP = pairs(lambda xh, z, core, xl, y: (xh, z, core, xl, y + 1 - 2 * core))
Y_DOWN = pairs(lambda xh, z, core, xl, y: (xh, z, core, xl, y - 1 + 2 * core))
Z_UP = pairs(lambda xh, z, core, xl, y: (xh, z + 1 - 2 * core, core, xl, y))
Z_DOWN = pairs(lambda xh, z, core, xl, y: (xh, z - 1 + 2 * core, core, xl, y))
X_LO = pairs(lambda xh, z, core, xl, y: (xh, z, core, xl + 1, y))
X_HI = pairs(lambda xh, z, core, xl, y: (xh + 1, z, core, xl, y))
CORE = pairs(lambda xh, z, core, xl, y: (xh, z, core + 1, xl, y))


def piece(flip, steps, core):
    up = 1 - 2 * core
    return 4 * flip + {0: 0, -up % 4: 1, up % 4: 2, 2: 3}[steps % 4]


def table():
    rows = []
    for xh, z, core, xl, y in devices():
        far = (z + 2) % 4
        last = (1 - xh) * 4 + far
        order = [xl * 4 + k for k in range(4) if k != far]
        order.append(xl * 4 + far if xl == xh else (1 - xl) * 4 + y)
        order += [k for k in range(8) if k not in order + [last]] + [last]
        left = [piece(k // 4 ^ xl, k % 4 - y, core) for k in order]
        mine = [piece(k // 4 ^ xh, k % 4 - z, core) for k in order]
        other = [piece(k // 4 ^ xh, k % 4 - z, 1 - core) for k in order]
        rows.append(left + mine + other + [core] + [0] * 7)
    return np.array(rows, np.int32)


TABLE = table()


def send(value, where):
    return lax.ppermute(value, AXES, where)


def start_copy(refs, low, which, target, sem):
    if len(refs) == 1:
        pltpu.make_async_copy(refs[0], target, sem).start()
        return
    half = len(refs) // 2
    lax.cond(
        which < low + half,
        lambda: start_copy(refs[:half], low, which, target, sem),
        lambda: start_copy(refs[half:], low + half, which, target, sem),
    )


def kernel(begin, groups, first, index_ref, *refs):
    left, mine, other = refs[0:8], refs[8:16], refs[16:24]
    refs = refs[24:]
    if not first:
        total_ref, refs = refs[0], refs[1:]
    out, a, b, sem_a, sem_b = refs[:5]
    acc = out if first else refs[5]
    core = index_ref[24]

    def issue(t, carry):
        at = pl.multiple_of(t * W, W)
        row = at + core * B
        far_row = at + (1 - core) * B
        start_copy(left, 0, index_ref[begin + t], a.at[:, pl.ds(at, W)], sem_a.at[t])
        start_copy(mine, 0, index_ref[8 + begin + t], b.at[pl.ds(pl.multiple_of(row, B), B)], sem_b.at[t])
        start_copy(other, 0, index_ref[16 + begin + t], b.at[pl.ds(pl.multiple_of(far_row, B), B)], sem_b.at[t])
        return carry

    lax.fori_loop(0, sum(groups), issue, 0)
    if not first:
        total = pltpu.make_async_copy(total_ref, acc, refs[6])
        total.start()
    t = 0
    for g, size in enumerate(groups):
        for u in range(t, t + size):
            x, y = a.at[:, pl.ds(u * W, W)], b.at[pl.ds(u * W, W)]
            pltpu.make_async_copy(x, x, sem_a.at[u]).wait()
            pltpu.make_async_copy(y, y, sem_b.at[u]).wait()
        x, y = a[:, t * W:(t + size) * W], b[t * W:(t + size) * W, :]
        part = jnp.dot(x, y, preferred_element_type=jnp.float32)
        t += size
        if g > 0:
            part = part + acc[...]
        elif not first:
            total.wait()
            part = part + acc[...]
        if g == len(groups) - 1:
            out[...] = part.astype(out.dtype)
        else:
            acc[...] = part


def multiply(stage, index, left, mine, other, total=None):
    groups = GROUPS[stage]
    begin = sum(sum(g) for g in GROUPS[:stage])
    first, last = stage == 0, stage == len(GROUPS) - 1
    block = pl.BlockSpec(memory_space=pltpu.VMEM)
    count = sum(groups)
    return pl.pallas_call(
        functools.partial(kernel, begin, groups, first),
        out_shape=jax.ShapeDtypeStruct((B, W), jnp.bfloat16 if last else jnp.float32),
        in_specs=[pl.BlockSpec(memory_space=pltpu.SMEM)]
        + [pl.BlockSpec(memory_space=pltpu.HBM)] * 24
        + [pl.BlockSpec(memory_space=pltpu.HBM)] * (not first),
        out_specs=block,
        scratch_shapes=[
            pltpu.VMEM((B, count * W), jnp.bfloat16),
            pltpu.VMEM((count * W, W), jnp.bfloat16),
            pltpu.SemaphoreType.DMA((count,)),
            pltpu.SemaphoreType.DMA((count,)),
        ]
        + [pltpu.VMEM((B, W), jnp.float32), pltpu.SemaphoreType.DMA] * (not first),
        compiler_params=pltpu.CompilerParams(vmem_limit_bytes=17 << 20),
        cost_estimate=pl.CostEstimate(
            flops=2 * B * W * W * sum(groups),
            bytes_accessed=3 * B * W * 2 * sum(groups),
            transcendentals=0,
        ),
    )(index, *left, *mine, *other, *([] if first else [total]))


def square(block, index):
    xl = send(block, X_LO)
    zu = send(block, Z_UP)
    zd = send(block, Z_DOWN)
    xh = send(block, X_HI)
    yu = send(block, Y_UP)
    yd = send(block, Y_DOWN)
    pyu = send(xl, Y_UP)
    pyd = send(xl, Y_DOWN)
    zf = send(zu, Z_UP)
    yf = send(yu, Y_UP)
    pzu = send(xh, Z_UP)
    pzd = send(xh, Z_DOWN)
    pyf = send(yf, X_LO)
    pzf = send(pzu, Z_UP)
    left = [block, yu, yd, yf, xl, pyu, pyd, pyf]
    mine = [block, zu, zd, zf, xh, pzu, pzd, pzf]
    other = [send(v, CORE) for v in mine]
    now = [v[:3] + [block] + v[4:7] + [block] for v in (mine, other)]
    soon = [v[:7] + [block] for v in (mine, other)]
    total = multiply(0, index, left[:4] + [block] * 4, *now)
    total = multiply(1, index, left[:5] + [block] * 3, *soon, total)
    total = multiply(2, index, left, *soon, total)
    return multiply(3, index, left, mine, other, total)


def body(approximant):
    index = jnp.asarray(TABLE)[lax.axis_index("row") * 8 + lax.axis_index("col")]
    squared = square(approximant, index)
    fourth_power = square(squared, index)
    return (squared, fourth_power)


def solution(mesh):
    return jax.shard_map(
        body,
        mesh=mesh,
        in_specs=(P("row", "col"),),
        out_specs=(P("row", "col"), P("row", "col")),
        check_vma=False,
    )
```

```python
import functools

import jax
import jax.numpy as jnp
import numpy as np
from jax import lax
from jax.experimental import pallas as pl
from jax.experimental.pallas import tpu as pltpu
from jax.sharding import PartitionSpec as P


AXES = ("row", "col")
B = 448
W = 896
GROUPS = ((1, 2), (1,), (1, 2), (1,))


def devices():
    for xh in range(2):
        for z in range(4):
            for core in range(2):
                for xl in range(2):
                    for y in range(4):
                        yield xh, z, core, xl, y


def pairs(move):
    out = []
    for source, place in enumerate(devices()):
        xh, z, core, xl, y = move(*place)
        out.append((source, (((xh % 2) * 4 + z % 4) * 2 + core % 2) * 8 + (xl % 2) * 4 + y % 4))
    return out


Y_UP = pairs(lambda xh, z, core, xl, y: (xh, z, core, xl, y + 1 - 2 * core))
Y_DOWN = pairs(lambda xh, z, core, xl, y: (xh, z, core, xl, y - 1 + 2 * core))
Z_UP = pairs(lambda xh, z, core, xl, y: (xh, z + 1 - 2 * core, core, xl, y))
Z_DOWN = pairs(lambda xh, z, core, xl, y: (xh, z - 1 + 2 * core, core, xl, y))
X_LO = pairs(lambda xh, z, core, xl, y: (xh, z, core, xl + 1, y))
X_HI = pairs(lambda xh, z, core, xl, y: (xh + 1, z, core, xl, y))
CORE = pairs(lambda xh, z, core, xl, y: (xh, z, core + 1, xl, y))


def piece(flip, steps, core):
    up = 1 - 2 * core
    return 4 * flip + {0: 0, -up % 4: 1, up % 4: 2, 2: 3}[steps % 4]


def table():
    rows = []
    for xh, z, core, xl, y in devices():
        far = (z + 2) % 4
        last = (1 - xh) * 4 + far
        order = [xl * 4 + k for k in range(4) if k != far]
        order.append(xl * 4 + far if xl == xh else (1 - xl) * 4 + y)
        order += [k for k in range(8) if k not in order + [last]] + [last]
        left = [piece(k // 4 ^ xl, k % 4 - y, core) for k in order]
        mine = [piece(k // 4 ^ xh, k % 4 - z, core) for k in order]
        other = [piece(k // 4 ^ xh, k % 4 - z, 1 - core) for k in order]
        rows.append(left + mine + other + [core] + [0] * 7)
    return np.array(rows, np.int32)


TABLE = table()


def send(value, where):
    return lax.ppermute(value, AXES, where)


def start_copy(refs, low, which, target, sem):
    if len(refs) == 1:
        pltpu.make_async_copy(refs[0], target, sem).start()
        return
    half = len(refs) // 2
    lax.cond(
        which < low + half,
        lambda: start_copy(refs[:half], low, which, target, sem),
        lambda: start_copy(refs[half:], low + half, which, target, sem),
    )


def kernel(begin, groups, first, index_ref, *refs):
    left, mine, other = refs[0:8], refs[8:16], refs[16:24]
    refs = refs[24:]
    if not first:
        total_ref, refs = refs[0], refs[1:]
    out, a, b, sem_a, sem_b = refs[:5]
    acc = out if first else refs[5]
    core = index_ref[24]

    def issue(t, carry):
        at = pl.multiple_of(t * W, W)
        row = at + core * B
        far_row = at + (1 - core) * B
        start_copy(left, 0, index_ref[begin + t], a.at[:, pl.ds(at, W)], sem_a.at[t])
        start_copy(mine, 0, index_ref[8 + begin + t], b.at[pl.ds(pl.multiple_of(row, B), B)], sem_b.at[t])
        start_copy(other, 0, index_ref[16 + begin + t], b.at[pl.ds(pl.multiple_of(far_row, B), B)], sem_b.at[t])
        return carry

    lax.fori_loop(0, sum(groups), issue, 0)
    if not first:
        total = pltpu.make_async_copy(total_ref, acc, refs[6])
        total.start()
    t = 0
    for g, size in enumerate(groups):
        for u in range(t, t + size):
            x, y = a.at[:, pl.ds(u * W, W)], b.at[pl.ds(u * W, W)]
            pltpu.make_async_copy(x, x, sem_a.at[u]).wait()
            pltpu.make_async_copy(y, y, sem_b.at[u]).wait()
        x, y = a[:, t * W:(t + size) * W], b[t * W:(t + size) * W, :]
        part = jnp.dot(x, y, preferred_element_type=jnp.float32)
        t += size
        if g > 0:
            part = part + acc[...]
        elif not first:
            total.wait()
            part = part + acc[...]
        if g == len(groups) - 1:
            out[...] = part.astype(out.dtype)
        else:
            acc[...] = part


def multiply(stage, index, left, mine, other, total=None):
    groups = GROUPS[stage]
    begin = sum(sum(g) for g in GROUPS[:stage])
    first, last = stage == 0, stage == len(GROUPS) - 1
    block = pl.BlockSpec(memory_space=pltpu.VMEM)
    count = sum(groups)
    return pl.pallas_call(
        functools.partial(kernel, begin, groups, first),
        out_shape=jax.ShapeDtypeStruct((B, W), jnp.bfloat16 if last else jnp.float32),
        in_specs=[pl.BlockSpec(memory_space=pltpu.SMEM)]
        + [pl.BlockSpec(memory_space=pltpu.HBM)] * 24
        + [pl.BlockSpec(memory_space=pltpu.HBM)] * (not first),
        out_specs=block,
        scratch_shapes=[
            pltpu.VMEM((B, count * W), jnp.bfloat16),
            pltpu.VMEM((count * W, W), jnp.bfloat16),
            pltpu.SemaphoreType.DMA((count,)),
            pltpu.SemaphoreType.DMA((count,)),
        ]
        + [pltpu.VMEM((B, W), jnp.float32), pltpu.SemaphoreType.DMA] * (not first),
        compiler_params=pltpu.CompilerParams(vmem_limit_bytes=17 << 20),
        cost_estimate=pl.CostEstimate(
            flops=2 * B * W * W * sum(groups),
            bytes_accessed=3 * B * W * 2 * sum(groups),
            transcendentals=0,
        ),
    )(index, *left, *mine, *other, *([] if first else [total]))


def square(block, index, held):
    xl = send(block, X_LO)
    zu = send(block, Z_UP)
    zd = send(block, Z_DOWN)
    xh = send(block, X_HI)
    yu = send(held, Y_UP)
    yd = send(held, Y_DOWN)
    pyu = send(xl, Y_UP)
    pyd = send(xl, Y_DOWN)
    zf = send(zu, Z_UP)
    yf = send(yu, Y_UP)
    pzu = send(xh, Z_UP)
    pzd = send(xh, Z_DOWN)
    pyf = send(yf, X_LO)
    pzf = send(pzu, Z_UP)
    block = held
    left = [held, yu, yd, yf, xl, pyu, pyd, pyf]
    mine = [held, zu, zd, zf, xh, pzu, pzd, pzf]
    other = [send(v, CORE) for v in mine]
    now = [v[:3] + [held] + v[4:7] + [held] for v in (mine, other)]
    soon = [v[:7] + [held] for v in (mine, other)]
    total = multiply(0, index, left[:4] + [held] * 4, *now)
    total = multiply(1, index, left[:5] + [held] * 3, *soon, total)
    total = multiply(2, index, left, *soon, total)
    return multiply(3, index, left, mine, other, total)


def body(approximant):
    index = jnp.asarray(TABLE)[lax.axis_index("row") * 8 + lax.axis_index("col")]
    held = approximant + jnp.minimum(index[31], 0).astype(jnp.bfloat16)
    squared = square(approximant, index, held)
    fourth_power = square(squared, index, squared)
    return (squared, fourth_power)


def solution(mesh):
    return jax.shard_map(
        body,
        mesh=mesh,
        in_specs=(P("row", "col"),),
        out_specs=(P("row", "col"), P("row", "col")),
        check_vma=False,
    )
```
